32 devices in a mesh: expert: 16 (over z, y, x), dp: 2 (over core).
Axes of the slice: x: 2, y: 2, z: 4, core: 2. Of those that a mesh axis runs over, the one named last changes fastest.
Arguments:
- tokens: bfloat16 [4096, 3584], P('expert'), may hold values from -6 to 6
- expert_ids: int32 [4096, 8], P('expert'), may hold values from 0 to 255, all different within a row; in each aligned block of 256 rows (0 to 255, 256 to 511, ...) at most 16 rows name the same one
- gate_values: float32 [4096, 8], P('expert'), may hold values from 0.1 to 1
- tiles: int32 [16], P('expert'), may hold values from 1 to 2
- w_gate: bfloat16 [16, 3584, 2048], P('expert', None, 'dp'), may hold values from -0.09375 to 0.09375
- w_up: bfloat16 [16, 3584, 2048], P('expert', None, 'dp'), may hold values from -0.09375 to 0.09375
- w_down: bfloat16 [16, 2048, 3584], P('expert', 'dp'), may hold values from -0.125 to 0.125
- grad_out: bfloat16 [4096, 3584], P('expert', 'dp'), may hold values from -6 to 6
Outputs:
- mixed: bfloat16 [4096, 3584], P('expert', 'dp')
- grad_tokens: bfloat16 [4096, 3584], P('expert', 'dp')
- grad_gates: float32 [4096, 8], P('expert')
- grad_w_gate: bfloat16 [16, 3584, 2048], P('expert', None, 'dp')
- grad_w_up: bfloat16 [16, 3584, 2048], P('expert', None, 'dp')
- grad_w_down: bfloat16 [16, 2048, 3584], P('expert', 'dp')
The draws below stay inside these ranges and needn't reach their ends.
Inputs may be any that keep to these rules, and one draw needn't show every extreme that they name: `expert_ids`: each row names 8 different experts. Within the rows of one device (aligned blocks of 256 rows) no expert is named by more than 16 rows.
All inputs are finite; a program needn't handle non-finite values.
Results may differ from the reference program's by a relative error of at most 0.015.
Values may be sent and summed in bfloat16 or wider, within the bound.
No kernel may reach another device: no remote copies, remote signals or barrier semaphores. Data moves between devices by JAX's collectives and lax.ppermute only.
A program may use at most 128 MiB of HBM per device.

```python
import math
import jax
import jax.numpy as jnp
import numpy as np
from jax import lax

D = 3584
FF = 2048
ALL_EXPERTS = 256
TOP = 8
TILE = 128
TOK_DEV = 256
SLOTS = 16
EXPERTS = 16
TOKENS = 4096
N_EXPERT = 16


def touch_ends(values, key, least, top_value):
    dims = values.shape
    spot = [jax.random.randint(jax.random.fold_in(key, axis), (), 0, dims[axis]) for axis in range(len(dims))]
    values = values.at[tuple(spot)].set(least)
    longest = dims.index(max(dims))
    spot[longest] = (spot[longest] + 1) % dims[longest]
    return values.at[tuple(spot)].set(top_value)


def block_scale(key, shape, shards, least, largest):
    factor_of, own = 1.0, jax.random.fold_in(key, 6)
    for dim, parts in shards:
        heights = jnp.exp(jax.random.uniform(jax.random.fold_in(own, dim), (parts,), jnp.float32, least / len(shards), largest / len(shards)))
        factor_of = factor_of * jnp.repeat(heights, shape[dim] // parts).reshape([-1 if axis == dim else 1 for axis in range(len(shape))])
    return factor_of


def shared_out(own_key, own, number, rows, count, top, bound, skew):
    order = jax.random.permutation(own_key, count)
    packed, common = load_shares(count, rows * top, bound, skew, True), load_shares(count, rows * top, bound, skew, False)
    places = jnp.arange(count)

    def named(tallies, offset_by):
        used = int((tallies > 0).sum())
        fixed = max(1, used // 4)
        shifted = fixed + (places - fixed + offset_by * (used - fixed)) % max(1, count - fixed)
        return jnp.zeros((count,), jnp.int32).at[order[jnp.where(places < fixed, places, shifted)]].set(jnp.asarray(tallies, jnp.int32))

    tallies = jnp.where(number % 4 == 0, named(packed, number // 4), named(common, number - number // 4 - 1))
    mixed = jax.random.permutation(jax.random.fold_in(own, 3), count)
    source_of, receiver = mixed[0:count // 2 * 2:2], mixed[1:count // 2 * 2:2]
    margin = jnp.minimum(tallies[source_of] - 1, bound - tallies[receiver]) // 2
    margin = jnp.where((source_of == order[0]) | (receiver == order[0]) | (tallies[receiver] == 0), 0, jnp.maximum(margin, 0))
    shifted = jax.random.randint(jax.random.fold_in(own, 4), (count // 2,), 0, 1 << 20) % (margin + 1)
    tallies = tallies.at[source_of].add(-shifted).at[receiver].add(shifted)
    members = jnp.searchsorted(jnp.cumsum(tallies), jnp.arange(rows * top), side="right").astype(jnp.int32)
    table = members.reshape(top, rows).T
    table = table[jax.random.permutation(jax.random.fold_in(own, 1), rows)]
    offset_by = jax.random.randint(jax.random.fold_in(own, 2), (rows, 1), 0, top)
    return jnp.take_along_axis(table, (jnp.arange(top)[None, :] + offset_by) % top, axis=1)


def load_shares(number_of, total, most, slope, full):
    weights = [(1 << 20) // math.isqrt(standing ** slope) + 1 for standing in range(1, number_of + 1)]
    largest = most if full else min(most, max(-(-total // number_of), total * weights[0] // sum(weights)))
    least = 1 if total - largest >= number_of - 1 else 0
    counts, surplus = [largest] + [least] * (number_of - 1), total - largest - least * (number_of - 1)
    while surplus > 0:
        movable = [i for i in range(1, number_of) if counts[i] < largest] or [i for i in range(1, number_of) if counts[i] < most]
        pool, budget = sum([weights[i] for i in movable]), surplus
        for i in movable:
            addition = min(most - counts[i], max(1, budget * weights[i] // pool), surplus)
            counts[i] = counts[i] + addition
            surplus = surplus - addition
    return np.array(counts)


def noise(rng, shape, spread, most, cuts=(), kind=jnp.bfloat16):
    result = jax.random.normal(rng, shape, jnp.float32) * spread
    if len(cuts) > 0:
        result = block_scale(rng, shape, cuts, -0.22, 0.18) * result
    return jnp.clip(result, min=-most, max=most).astype(kind)


def setup_inputs(seed: int = 0) -> dict:
    key_of = jax.random.split(jax.random.key(seed), 9)
    tokens = noise(key_of[0], (TOKENS, D), 1.0, 6.0, ((0, 16),))
    expert_ids_keys = jax.random.split(jax.random.fold_in(key_of[1], 1), TOKENS // TOK_DEV)
    expert_ids_turns = jax.random.permutation(jax.random.fold_in(key_of[1], 3), TOKENS // TOK_DEV)
    expert_ids = jax.vmap(lambda own, number: shared_out(jax.random.fold_in(key_of[1], 2), own, number, TOK_DEV, ALL_EXPERTS, TOP, SLOTS, 2))(expert_ids_keys, expert_ids_turns).reshape((TOKENS, TOP))
    gate_values = jnp.clip(0.1 + 0.9 * jax.random.uniform(key_of[2], (TOKENS, TOP), jnp.float32) ** block_scale(key_of[2], (TOKENS, TOP), ((0, 16),), -0.2, 0.2), 0.1, 1.0)
    tiles = touch_ends(jax.random.randint(key_of[3], (N_EXPERT,), 1, TOK_DEV // TILE + 1), jax.random.fold_in(key_of[3], 1), 1, (TOK_DEV // TILE + 1) - 1).astype(jnp.int32)
    w_gate = noise(key_of[4], (EXPERTS, D, FF), D ** -0.5, 0.09375, ((0, 16), (2, 2)))
    w_up = noise(key_of[5], (EXPERTS, D, FF), D ** -0.5, 0.09375, ((0, 16), (2, 2)))
    w_down = noise(key_of[6], (EXPERTS, FF, D), FF ** -0.5, 0.125, ((0, 16), (1, 2)))
    grad_out = noise(key_of[7], (TOKENS, D), 1.0, 6.0, ((0, 16), (1, 2)))
    return dict(tokens=tokens, expert_ids=expert_ids, gate_values=gate_values, tiles=tiles, w_gate=w_gate, w_up=w_up, w_down=w_down, grad_out=grad_out)


def route_tables(ids, gates, count, experts, slots, tile):
    tok, top = ids.shape
    queue = experts * slots
    live = jnp.arange(tok, dtype=jnp.int32) < count * tile
    valid = (ids < experts) & live[:, None]
    flat_ids = ids.reshape(-1)
    flat_valid = valid.reshape(-1)
    onehot = ((flat_ids[:, None] == jnp.arange(experts, dtype=jnp.int32)[None, :]) & flat_valid[:, None]).astype(jnp.int32)
    ranks = jnp.sum((jnp.cumsum(onehot, axis=0).astype(jnp.int32) - 1) * onehot, axis=1).astype(jnp.int32)
    target = jnp.where(flat_valid, flat_ids * slots + ranks, -1).astype(jnp.int32)
    match = (target[None, :] == jnp.arange(queue, dtype=jnp.int32)[:, None]).astype(jnp.float32)
    picker = jnp.sum(match.reshape(queue, tok, top), axis=2)
    slot_gate = jnp.dot(match, gates.reshape(-1), precision=lax.Precision.HIGHEST)
    return match, picker, slot_gate


def reference(tokens, expert_ids, gate_values, tiles, w_gate, w_up, w_down, grad_out):
    experts = N_EXPERT
    queue = experts * SLOTS
    ids_b = expert_ids.reshape(experts, TOK_DEV, TOP)
    gates_b = gate_values.reshape(experts, TOK_DEV, TOP)
    tok_b = tokens.reshape(experts, TOK_DEV, D)
    dy_b = grad_out.reshape(experts, TOK_DEV, D)

    def gather_source(args):
        ids, gates, count, xs, dys = args
        match, picker, slot_gate = route_tables(ids, gates, count, experts, SLOTS, TILE)
        pick_b = picker.astype(jnp.bfloat16)
        xrows = jnp.dot(pick_b, xs, preferred_element_type=jnp.float32).astype(jnp.bfloat16)
        dy_rows = jnp.dot(pick_b, dys, preferred_element_type=jnp.float32)
        dyrow = (dy_rows * slot_gate[:, None]).astype(jnp.bfloat16)
        return xrows, dyrow

    xrows, dyrows = lax.map(gather_source, (ids_b, gates_b, tiles, tok_b, dy_b))

    def by_expert(a):
        return a.reshape(experts, experts, SLOTS, D).transpose(1, 0, 2, 3).reshape(experts, experts * SLOTS, D)

    def by_source(a):
        return a.reshape(experts, experts, SLOTS, D).transpose(1, 0, 2, 3).reshape(experts, queue, D)

    def one_expert(args):
        rows, dyr, wg, wu, wd = args
        gate_pre = jnp.dot(rows, wg, preferred_element_type=jnp.float32)
        up_pre = jnp.dot(rows, wu, preferred_element_type=jnp.float32)
        sig = jax.nn.sigmoid(gate_pre)
        hidden = (gate_pre * sig * up_pre).astype(jnp.bfloat16)
        yrow = jnp.dot(hidden, wd, preferred_element_type=jnp.float32)
        dh = jnp.dot(dyr, wd.T, preferred_element_type=jnp.float32)
        d_gate = (dh * up_pre * sig * (1.0 + gate_pre * (1.0 - sig))).astype(jnp.bfloat16)
        d_up = (dh * gate_pre * sig).astype(jnp.bfloat16)
        grad_down = jnp.dot(hidden.T, dyr, preferred_element_type=jnp.float32).astype(jnp.bfloat16)
        grad_gate = jnp.dot(rows.T, d_gate, preferred_element_type=jnp.float32).astype(jnp.bfloat16)
        grad_up = jnp.dot(rows.T, d_up, preferred_element_type=jnp.float32).astype(jnp.bfloat16)
        dxrow = jnp.dot(d_gate, wg.T, preferred_element_type=jnp.float32) + jnp.dot(d_up, wu.T, preferred_element_type=jnp.float32)
        return yrow, dxrow, grad_gate, grad_up, grad_down

    yrow, dxrow, grad_w_gate, grad_w_up, grad_w_down = lax.map(one_expert, (by_expert(xrows), by_expert(dyrows), w_gate, w_up, w_down))
    yrow = by_source(yrow)
    dxrow = by_source(dxrow)

    def combine(args):
        ids, gates, count, dys, ys, dxs = args
        match, picker, slot_gate = route_tables(ids, gates, count, experts, SLOTS, TILE)
        weighted = (picker * slot_gate[:, None]).T
        mixed = jnp.dot(weighted, ys, precision=lax.Precision.HIGHEST).astype(jnp.bfloat16)
        dy_rows = jnp.dot(picker.astype(jnp.bfloat16), dys, preferred_element_type=jnp.float32)
        score = jnp.sum(dy_rows * ys, axis=1)
        grad_gates = jnp.dot(score, match, precision=lax.Precision.HIGHEST).reshape(TOK_DEV, TOP)
        grad_tokens = jnp.dot(picker.T, dxs, precision=lax.Precision.HIGHEST).astype(jnp.bfloat16)
        return mixed, grad_tokens, grad_gates

    mixed, grad_tokens, grad_gates = lax.map(combine, (ids_b, gates_b, tiles, dy_b, yrow, dxrow))
    return (mixed.reshape(TOKENS, D), grad_tokens.reshape(TOKENS, D), grad_gates.reshape(TOKENS, TOP),
            grad_w_gate, grad_w_up, grad_w_down)
```

```python
import functools
import math

import jax
import jax.numpy as jnp
from jax import lax
from jax.experimental import pallas as pl
from jax.experimental.pallas import tpu as pltpu
from jax.sharding import PartitionSpec as P


TILE = 128
SLOTS = 16
F32 = jnp.float32
BF16 = jnp.bfloat16
VMEM = pl.BlockSpec(memory_space=pltpu.VMEM)
ANY = pl.BlockSpec(memory_space=pl.ANY)
SMEM = pl.BlockSpec(memory_space=pltpu.SMEM)
STEP = 256
PARTS = 4
DMAS = pltpu.SemaphoreType.DMA((PARTS,))


def params(mib):
    return pltpu.CompilerParams(vmem_limit_bytes=mib << 20)


def cost(flops, moved):
    return pl.CostEstimate(flops=flops, bytes_accessed=moved, transcendentals=0)


def dot_nn(a, b):
    return jnp.dot(a, b, preferred_element_type=F32)


def dot_nt(a, b):
    return lax.dot_general(a, b, (((1,), (1,)), ((), ())), preferred_element_type=F32)


def dot_tn(a, b):
    return lax.dot_general(a, b, (((0,), (0,)), ((), ())), preferred_element_type=F32)


def dispatch_kernel(where_ref, ids_ref, gates_ref, tok_ref, send_ref, pick_ref, weight_ref):
    top, tok = ids_ref.shape
    queue = pick_ref.shape[0]
    owner = lax.broadcasted_iota(jnp.int32, (queue, tok), 0)
    expert, slot = owner // SLOTS, owner % SLOTS
    ids, gates = ids_ref[...], gates_ref[...]
    named = jnp.zeros((queue, tok), F32)
    weight = jnp.zeros((queue, tok), F32)
    for k in range(top):
        hit = jnp.broadcast_to(ids[k : k + 1, :], (queue, tok)) == expert
        named = jnp.where(hit, 1.0, named)
        weight = jnp.where(hit, jnp.broadcast_to(gates[k : k + 1, :], (queue, tok)), weight)
    live = lax.broadcasted_iota(jnp.int32, (queue, tok), 1) < where_ref[1] * TILE
    named = jnp.where(live, named, 0.0)
    before = lax.broadcasted_iota(jnp.int32, (tok, tok), 0) < lax.broadcasted_iota(
        jnp.int32, (tok, tok), 1
    )
    rank = dot_nn(named.astype(BF16), jnp.where(before, 1.0, 0.0).astype(BF16))
    chosen = (named > 0.5) & (rank == slot.astype(F32))
    pick = jnp.where(chosen, 1.0, 0.0).astype(BF16)
    send_ref[...] = dot_nn(pick, tok_ref[...]).astype(BF16)
    pick_ref[...] = pick
    weight_ref[...] = jnp.where(chosen, weight, 0.0)


def cotangent_kernel(pick_ref, weight_ref, out_ref, send_ref):
    gate = jnp.sum(weight_ref[...], axis=1, keepdims=True)
    send_ref[...] = (dot_nn(pick_ref[...], out_ref[...]) * gate).astype(BF16)


def combine_kernel(pick_ref, weight_ref, ids_ref, back_ref, out_ref, mixed_ref, score_ref):
    back = back_ref[...]
    weight = weight_ref[...]
    upper = weight.astype(BF16)
    lower = (weight - upper.astype(F32)).astype(BF16)
    mixed_ref[...] = (dot_tn(upper, back) + dot_tn(lower, back)).astype(BF16)
    pairs = dot_nt(back, out_ref[...])
    pairs = jnp.where(pick_ref[...] > 0.5, pairs, 0.0)
    queue, tok = pairs.shape
    expert = lax.broadcasted_iota(jnp.int32, (queue, tok), 0) // SLOTS
    ids = ids_ref[...]
    for k in range(ids.shape[0]):
        hit = jnp.broadcast_to(ids[k : k + 1, :], (queue, tok)) == expert
        score_ref[k : k + 1, :] = jnp.sum(jnp.where(hit, pairs, 0.0), axis=0, keepdims=True)


def spread_kernel(pick_ref, back_ref, out_ref):
    out_ref[...] = dot_tn(pick_ref[...], back_ref[...]).astype(BF16)


def fetch(src, dst, sems):
    rows = src.shape[0] // PARTS
    return [
        pltpu.make_async_copy(src.at[pl.ds(i * rows, rows)], dst.at[pl.ds(i * rows, rows)], sems.at[i])
        for i in range(PARTS)
    ]


def begin(copies):
    for copy in copies:
        copy.start()


def finish(copies):
    for copy in copies:
        copy.wait()


def load_kernel(*refs):
    n = len(refs) // 3
    copies = []
    for src, dst, sems in zip(refs[:n], refs[n : 2 * n], refs[2 * n :]):
        copies += fetch(src, dst, sems)
    begin(copies)
    finish(copies)


def enter_kernel(part_ref, x_ref, wg_ref, wu_ref, next_ref, g_ref, u_ref, kept_ref, sems):
    copies = fetch(next_ref, kept_ref, sems)
    begin(copies)
    k = x_ref.shape[1]
    first = pl.multiple_of(part_ref[0] * k, 128)
    for j in range(0, g_ref.shape[1], STEP):
        c = slice(j, j + STEP)
        g_ref[:, c] = dot_nn(x_ref[...], wg_ref[pl.ds(first, k), c])
        u_ref[:, c] = dot_nn(x_ref[...], wu_ref[pl.ds(first, k), c])
    finish(copies)


def hidden_kernel(part_ref, x_ref, wg_ref, wu_ref, g0_ref, u0_ref, h_ref, a_ref, b_ref):
    k = x_ref.shape[1]
    first = pl.multiple_of(part_ref[0] * k, 128)
    for j in range(0, h_ref.shape[1], STEP):
        c = slice(j, j + STEP)
        g = g0_ref[:, c] + dot_nn(x_ref[...], wg_ref[pl.ds(first, k), c])
        u = u0_ref[:, c] + dot_nn(x_ref[...], wu_ref[pl.ds(first, k), c])
        sig = jax.nn.sigmoid(g)
        gated = g * sig
        h_ref[:, c] = (gated * u).astype(BF16)
        a_ref[:, c] = (u * sig * (1.0 + g * (1.0 - sig))).astype(BF16)
        b_ref[:, c] = gated.astype(BF16)


def leave_kernel(part_ref, h_ref, w_ref, y_ref):
    n = y_ref.shape[1]
    first = part_ref[0] * n
    for j in range(0, n, STEP):
        cols = pl.ds(pl.multiple_of(first + j, 128), STEP)
        y_ref[:, j : j + STEP] = dot_nn(h_ref[...], w_ref[:, cols]).astype(y_ref.dtype)


def back_kernel(part_ref, dy_ref, w_ref, ng_ref, nu_ref, dh_ref, kg_ref, ku_ref, g_sems, u_sems):
    copies = fetch(ng_ref, kg_ref, g_sems) + fetch(nu_ref, ku_ref, u_sems)
    begin(copies)
    k = dy_ref.shape[1]
    cols = pl.ds(pl.multiple_of(part_ref[0] * k, 128), k)
    for j in range(0, dh_ref.shape[1], STEP):
        dh_ref[:, j : j + STEP] = dot_nt(dy_ref[...], w_ref[j : j + STEP, cols])
    finish(copies)


def inner_kernel(part_ref, dy_ref, w_ref, dh0_ref, a_ref, b_ref, dg_ref, du_ref):
    k = dy_ref.shape[1]
    cols = pl.ds(pl.multiple_of(part_ref[0] * k, 128), k)
    for j in range(0, dg_ref.shape[1], STEP):
        c = slice(j, j + STEP)
        dh = dh0_ref[:, c] + dot_nt(dy_ref[...], w_ref[c, cols])
        dg_ref[:, c] = (dh * a_ref[:, c].astype(F32)).astype(BF16)
        du_ref[:, c] = (dh * b_ref[:, c].astype(F32)).astype(BF16)


def input_kernel(part_ref, dg_ref, du_ref, wg_ref, wu_ref, dx_ref):
    n = dx_ref.shape[1]
    first = part_ref[0] * n
    for j in range(0, n, STEP):
        rows = pl.ds(pl.multiple_of(first + j, 128), STEP)
        dx_ref[:, j : j + STEP] = (
            dot_nt(dg_ref[...], wg_ref[rows, :]) + dot_nt(du_ref[...], wu_ref[rows, :])
        ).astype(dx_ref.dtype)


def in_hbm(x):
    return pltpu.with_memory_space_constraint(x, pltpu.HBM)


def call(kernel, outs, *args, specs=None, scratch=(), flops=0, mib=6):
    shapes = [(pltpu.VMEM if kept else jax.ShapeDtypeStruct)(s, d) for s, d, kept in outs]
    moved = sum(a.size * a.dtype.itemsize for a in args) + sum(
        math.prod(s) * jnp.dtype(d).itemsize for s, d, _ in outs
    )
    result = pl.pallas_call(
        kernel,
        in_specs=specs or [SMEM] + [VMEM] * (len(args) - 1),
        out_specs=[VMEM] * len(shapes),
        out_shape=shapes,
        scratch_shapes=list(scratch),
        compiler_params=params(mib),
        cost_estimate=cost(flops, moved),
    )(*args)
    return result if len(shapes) > 1 else result[0]


def load(*arrays):
    kept = call(
        load_kernel, [(a.shape, a.dtype, True) for a in arrays], *arrays,
        specs=[ANY] * len(arrays), scratch=[DMAS] * len(arrays),
    )
    return kept


def swap(x):
    return lax.ppermute(x, "dp", [(0, 1), (1, 0)])


def exchange(x, experts):
    rows, width = x.shape
    x = lax.all_to_all(
        x.reshape(experts, rows // experts, width), "expert", 0, 0, tiled=True
    )
    return x.reshape(rows, width)


def paired(tokens, expert_ids, gate_values, tiles, w_gate, w_up, w_down, grad_out):
    experts = lax.axis_size("expert")
    tok, width = tokens.shape
    top = expert_ids.shape[1]
    queue = experts * SLOTS
    half = width // 2
    wg, wu, wd = (in_hbm(w[0]) for w in (w_gate, w_up, w_down))
    hid = wg.shape[1]
    me = lax.axis_index("dp").astype(jnp.int32)
    mine = me.reshape(1)
    other = 1 - mine
    ids_t, gates_t = expert_ids.T, gate_values.T
    unit = 2 * queue * half * hid

    send, pick, weight = pl.pallas_call(
        dispatch_kernel,
        grid_spec=pltpu.PrefetchScalarGridSpec(
            num_scalar_prefetch=1,
            grid=(1,),
            in_specs=[
                pl.BlockSpec((top, tok), lambda i, s: (0, 0)),
                pl.BlockSpec((top, tok), lambda i, s: (0, 0)),
                pl.BlockSpec((tok, half), lambda i, s: (0, s[0])),
            ],
            out_specs=[
                pl.BlockSpec((queue, half), lambda i, s: (0, 0)),
                pl.BlockSpec((queue, tok), lambda i, s: (0, 0)),
                pl.BlockSpec((queue, tok), lambda i, s: (0, 0)),
            ],
        ),
        out_shape=[
            jax.ShapeDtypeStruct((queue, half), BF16),
            jax.ShapeDtypeStruct((queue, tok), BF16),
            jax.ShapeDtypeStruct((queue, tok), F32),
        ],
        compiler_params=params(8),
        name="dispatch",
    )(jnp.concatenate([mine, tiles]), in_hbm(ids_t), in_hbm(gates_t), in_hbm(tokens))
    x_own = exchange(send, experts)
    dy_send = call(
        cotangent_kernel, [((queue, half), BF16, False)], pick, weight, grad_out,
        specs=[VMEM] * 3, flops=2 * queue * tok * half,
    )
    dy_send, x_own = lax.optimization_barrier((dy_send, x_own))
    dy_own = exchange(dy_send, experts)

    inner = ((queue, hid), F32, True)
    x_oth = swap(x_own)
    wg0, wu0 = load(wg, wu)
    g0, u0, wd0 = call(
        enter_kernel, [inner, inner, (wd.shape, BF16, True)], mine, x_own, wg0, wu0, wd,
        specs=[SMEM] + [VMEM] * 3 + [ANY], scratch=[DMAS], flops=2 * unit,
    )
    h, a, b = call(
        hidden_kernel, [((queue, hid), BF16, False)] * 3, other, x_oth, wg0, wu0, g0, u0,
        flops=2 * unit,
    )
    y_far = call(leave_kernel, [((queue, half), BF16, False)], other, h, wd0, flops=unit)
    y_far = swap(y_far)
    y_near = call(leave_kernel, [((queue, half), F32, False)], mine, h, wd0, flops=unit)
    y_sum = (y_near + y_far.astype(F32)).astype(BF16)
    y_back = exchange(y_sum, experts)

    dy_oth = swap(dy_own)
    wd1 = load(wd)
    dh0, wg1, wu1 = call(
        back_kernel, [inner, (wg.shape, BF16, True), (wu.shape, BF16, True)], mine, dy_own, wd1, wg, wu,
        specs=[SMEM] + [VMEM] * 2 + [ANY] * 2, scratch=[DMAS] * 2, flops=unit,
    )
    dg, du = call(
        inner_kernel, [((queue, hid), BF16, False)] * 2, other, dy_oth, wd1, dh0, a, b,
        flops=unit,
    )
    dx_far = call(
        input_kernel, [((queue, half), BF16, False)], other, dg, du, wg1, wu1, flops=2 * unit
    )
    dx_far = swap(dx_far)
    dx_near = call(
        input_kernel, [((queue, half), F32, False)], mine, dg, du, wg1, wu1, flops=2 * unit
    )
    dx_sum = (dx_near + dx_far.astype(F32)).astype(BF16)
    dx_back = exchange(dx_sum, experts)

    first = me == 0
    x_full = jnp.where(
        first, jnp.concatenate([x_own, x_oth], 1), jnp.concatenate([x_oth, x_own], 1)
    )
    dy_full = jnp.where(
        first, jnp.concatenate([dy_own, dy_oth], 1), jnp.concatenate([dy_oth, dy_own], 1)
    )
    grad_down = dot_tn(h, dy_full).astype(BF16)
    grad_gate = dot_tn(x_full, dg).astype(BF16)
    grad_up = dot_tn(x_full, du).astype(BF16)

    mixed, score = call(
        combine_kernel, [((tok, half), BF16, False), ((top, tok), F32, False)],
        pick, weight, ids_t, y_back, grad_out,
        specs=[VMEM] * 5, flops=6 * queue * tok * half,
    )
    grad_gates = (score + swap(score)).T
    grad_tokens = call(
        spread_kernel, [((tok, half), BF16, False)], pick, dx_back,
        specs=[VMEM] * 2, flops=2 * queue * tok * half,
    )
    return mixed, grad_tokens, grad_gates, grad_gate[None], grad_up[None], grad_down[None]


def route_tables(ids, gates, count, experts, slots, tile):
    tok, top = ids.shape
    queue = experts * slots
    live = jnp.arange(tok, dtype=jnp.int32) < count * tile
    valid = (ids < experts) & live[:, None]
    flat_ids = ids.reshape(-1)
    flat_valid = valid.reshape(-1)
    onehot = (
        (flat_ids[:, None] == jnp.arange(experts, dtype=jnp.int32)[None, :]) & flat_valid[:, None]
    ).astype(jnp.int32)
    ranks = jnp.sum((jnp.cumsum(onehot, axis=0) - 1) * onehot, axis=1)
    target = jnp.where(flat_valid, flat_ids * slots + ranks, -1)
    match = (target[None, :] == jnp.arange(queue, dtype=jnp.int32)[:, None]).astype(F32)
    picker = jnp.sum(match.reshape(queue, tok, top), axis=2)
    slot_gate = jnp.dot(match, gates.reshape(-1), precision=lax.Precision.HIGHEST)
    return match, picker, slot_gate


def spread_rows(picker_tb, values):
    upper = values.astype(BF16)
    lower = (values - upper.astype(F32)).astype(BF16)
    return dot_nn(picker_tb, upper) + dot_nn(picker_tb, lower)


def shared(tokens, expert_ids, gate_values, tiles, w_gate, w_up, w_down, grad_out):
    experts = lax.axis_size("expert")
    groups = lax.axis_size("dp")
    tok, width = tokens.shape
    top = expert_ids.shape[1]
    columns = width // groups
    match, picker, slot_gate = route_tables(expert_ids, gate_values, tiles[0], experts, SLOTS, TILE)
    pick_b = picker.astype(BF16)
    picker_tb = picker.T.astype(BF16)
    mine = lax.dynamic_slice_in_dim(tokens, lax.axis_index("dp") * columns, columns, 1)
    rows = exchange(dot_nn(pick_b, mine).astype(BF16), experts)
    rows = lax.all_gather(rows, "dp", axis=1, tiled=True)
    w_g, w_u, w_d = w_gate[0], w_up[0], w_down[0]
    gate_pre = dot_nn(rows, w_g)
    up_pre = dot_nn(rows, w_u)
    sig = jax.nn.sigmoid(gate_pre)
    hidden = (gate_pre * sig * up_pre).astype(BF16)
    summed = lax.psum_scatter(
        dot_nn(hidden, w_d).astype(BF16), "dp", scatter_dimension=1, tiled=True
    )
    returned = exchange(summed, experts).astype(F32)
    mixed = spread_rows(picker_tb, returned * slot_gate[:, None]).astype(BF16)
    dy_rows = dot_nn(pick_b, grad_out)
    score = lax.psum(jnp.sum(dy_rows * returned, axis=1), "dp")
    dy_own = exchange((dy_rows * slot_gate[:, None]).astype(BF16), experts)
    dy_slots = lax.all_gather(dy_own, "dp", axis=1, tiled=True)
    d_hidden = dot_nt(dy_slots, w_d)
    d_gate = (d_hidden * up_pre * sig * (1.0 + gate_pre * (1.0 - sig))).astype(BF16)
    d_up = (d_hidden * gate_pre * sig).astype(BF16)
    grad_down = dot_tn(hidden, dy_slots).astype(BF16)
    grad_gate = dot_tn(rows, d_gate).astype(BF16)
    grad_up = dot_tn(rows, d_up).astype(BF16)
    input_rows = dot_nt(d_gate, w_g) + dot_nt(d_up, w_u)
    input_summed = lax.psum_scatter(
        input_rows.astype(BF16), "dp", scatter_dimension=1, tiled=True
    )
    grad_tokens = dot_nn(picker_tb, exchange(input_summed, experts)).astype(BF16)
    grad_gates = jnp.dot(score, match, precision=lax.Precision.HIGHEST).reshape(tok, top)
    return mixed, grad_tokens, grad_gates, grad_gate[None], grad_up[None], grad_down[None]


def in_pairs(mesh, width, hid):
    return mesh.shape["dp"] == 2 and width % (2 * STEP) == 0 and hid % (2 * STEP) == 0


def solution(mesh):
    placed = (
        P("expert", None),
        P("expert", None),
        P("expert", None),
        P("expert"),
        P("expert", None, "dp"),
        P("expert", None, "dp"),
        P("expert", "dp", None),
        P("expert", "dp"),
    )
    over = functools.partial(
        jax.shard_map,
        mesh=mesh,
        in_specs=placed,
        out_specs=(
            P("expert", "dp"),
            P("expert", "dp"),
            P("expert", None),
            P("expert", None, "dp"),
            P("expert", None, "dp"),
            P("expert", "dp", None),
        ),
        check_vma=False,
    )

    def layer(*args):
        if not in_pairs(mesh, *args[4].shape[1:]):
            return over(shared)(*args)
        return over(paired)(*args)

    return layer
```

```python
import functools
import math

import jax
import jax.numpy as jnp
from jax import lax
from jax.experimental import pallas as pl
from jax.experimental.pallas import tpu as pltpu
from jax.sharding import PartitionSpec as P


TILE = 128
SLOTS = 16
F32 = jnp.float32
BF16 = jnp.bfloat16
VMEM = pl.BlockSpec(memory_space=pltpu.VMEM)
ANY = pl.BlockSpec(memory_space=pl.ANY)
SMEM = pl.BlockSpec(memory_space=pltpu.SMEM)
STEP = 256
PARTS = 4
PIECES = 2
DMAS = pltpu.SemaphoreType.DMA((PARTS,))


def params(mib):
    return pltpu.CompilerParams(vmem_limit_bytes=mib << 20)


def cost(flops, moved):
    return pl.CostEstimate(flops=flops, bytes_accessed=moved, transcendentals=0)


def dot_nn(a, b):
    return jnp.dot(a, b, preferred_element_type=F32)


def dot_nt(a, b):
    return lax.dot_general(a, b, (((1,), (1,)), ((), ())), preferred_element_type=F32)


def dot_tn(a, b):
    return lax.dot_general(a, b, (((0,), (0,)), ((), ())), preferred_element_type=F32)


def pieces(src, dst, sems, src_first=0, dst_first=0):
    wide = min(src.shape[1], dst.shape[1]) // PIECES
    return [
        pltpu.make_async_copy(
            src.at[:, pl.ds(pl.multiple_of(src_first + i * wide, 128), wide)],
            dst.at[:, pl.ds(pl.multiple_of(dst_first + i * wide, 128), wide)],
            sems.at[i],
        )
        for i in range(PIECES)
    ]


def dispatch_kernel(
    part_ref, tiles_ref, ids_ref, gates_ref, tok_ref, send_ref, pick_ref, weight_ref,
    ids_v, gates_v, tok_v, send_v, pick_v, weight_v, near_s, in_s, out_s,
):
    top, tok = ids_v.shape
    queue, half = send_v.shape
    named_in = [
        pltpu.make_async_copy(ids_ref, ids_v, near_s.at[0]),
        pltpu.make_async_copy(gates_ref, gates_v, near_s.at[1]),
    ]
    tables = [
        pltpu.make_async_copy(pick_v, pick_ref, near_s.at[2]),
        pltpu.make_async_copy(weight_v, weight_ref, near_s.at[3]),
    ]
    ins = pieces(tok_ref, tok_v, in_s, part_ref[0] * half)
    outs = pieces(send_v, send_ref, out_s)
    begin(named_in + ins)
    owner = lax.broadcasted_iota(jnp.int32, (queue, tok), 0)
    expert, slot = owner // SLOTS, owner % SLOTS
    before = lax.broadcasted_iota(jnp.int32, (tok, tok), 0) < lax.broadcasted_iota(
        jnp.int32, (tok, tok), 1
    )
    earlier = jnp.where(before, 1.0, 0.0).astype(BF16)
    live = lax.broadcasted_iota(jnp.int32, (1, tok), 1) < tiles_ref[0] * TILE
    finish(named_in)
    ids = jnp.where(live, ids_v[...], -1)
    gates = gates_v[...]
    named = jnp.zeros((queue, tok), F32)
    weight = jnp.zeros((queue, tok), F32)
    for k in range(top):
        hit = jnp.broadcast_to(ids[k : k + 1, :], (queue, tok)) == expert
        named = jnp.where(hit, 1.0, named)
        weight = jnp.where(hit, jnp.broadcast_to(gates[k : k + 1, :], (queue, tok)), weight)
    rank = dot_nn(named.astype(BF16), earlier)
    chosen = (named > 0.5) & (rank == slot.astype(F32))
    pick = jnp.where(chosen, 1.0, 0.0).astype(BF16)
    pick_v[...] = pick
    weight_v[...] = jnp.where(chosen, weight, 0.0)
    begin(tables)
    wide = half // PIECES
    for i in range(PIECES):
        c = slice(i * wide, (i + 1) * wide)
        ins[i].wait()
        send_v[:, c] = dot_nn(pick, tok_v[:, c]).astype(BF16)
        outs[i].start()
    finish(outs + tables)


def cotangent_kernel(pick_ref, weight_ref, out_ref, send_ref):
    gate = jnp.sum(weight_ref[...], axis=1, keepdims=True)
    send_ref[...] = (dot_nn(pick_ref[...], out_ref[...]) * gate).astype(BF16)


def combine_kernel(
    pick_ref, weight_ref, ids_ref, back_ref, out_ref, mixed_ref, score_ref, back_v, mixed_v, in_s, out_s
):
    ins, outs = pieces(back_ref, back_v, in_s), pieces(mixed_v, mixed_ref, out_s)
    begin(ins)
    weight = weight_ref[...].T
    upper = weight.astype(BF16)
    lower = (weight - upper.astype(F32)).astype(BF16)
    wide = back_v.shape[1] // PIECES
    pairs = 0.0
    for i in range(PIECES):
        c = slice(i * wide, (i + 1) * wide)
        ins[i].wait()
        back = back_v[:, c]
        mixed_v[:, c] = (dot_nn(upper, back) + dot_nn(lower, back)).astype(BF16)
        outs[i].start()
        pairs += dot_nt(back, out_ref[:, c])
    pairs = jnp.where(pick_ref[...] > 0.5, pairs, 0.0)
    queue, tok = pairs.shape
    expert = lax.broadcasted_iota(jnp.int32, (queue, tok), 0) // SLOTS
    ids = ids_ref[...]
    for k in range(ids.shape[0]):
        hit = jnp.broadcast_to(ids[k : k + 1, :], (queue, tok)) == expert
        score_ref[k : k + 1, :] = jnp.sum(jnp.where(hit, pairs, 0.0), axis=0, keepdims=True)
    finish(outs)


def spread_kernel(pick_ref, back_ref, out_ref):
    out_ref[...] = dot_tn(pick_ref[...], back_ref[...]).astype(BF16)


def sum_kernel(near_ref, far_ref, out_ref):
    out_ref[...] = (near_ref[...] + far_ref[...].astype(F32)).astype(BF16)


def columns_kernel(part_ref, own_ref, oth_ref, dg_ref, du_ref, gate_ref, up_ref):
    def write(x):
        turned = x.T
        gate_ref[...] = dot_nn(turned, dg_ref[...]).astype(BF16)
        up_ref[...] = dot_nn(turned, du_ref[...]).astype(BF16)

    near = pl.program_id(0) < pl.num_programs(0) // 2

    @pl.when(near)
    def _():
        write(own_ref[...])

    @pl.when(jnp.logical_not(near))
    def _():
        write(oth_ref[...])


def rows_kernel(part_ref, own_ref, oth_ref, h_ref, down_ref):
    turned = h_ref[...].T
    near = pl.program_id(0) < pl.num_programs(0) // 2

    @pl.when(near)
    def _():
        down_ref[...] = dot_nn(turned, own_ref[...]).astype(BF16)

    @pl.when(jnp.logical_not(near))
    def _():
        down_ref[...] = dot_nn(turned, oth_ref[...]).astype(BF16)


def fetch(src, dst, sems):
    rows = src.shape[0] // PARTS
    return [
        pltpu.make_async_copy(src.at[pl.ds(i * rows, rows)], dst.at[pl.ds(i * rows, rows)], sems.at[i])
        for i in range(PARTS)
    ]


def begin(copies):
    for copy in copies:
        copy.start()


def finish(copies):
    for copy in copies:
        copy.wait()


def load_kernel(*refs):
    n = len(refs) // 3
    copies = []
    for src, dst, sems in zip(refs[:n], refs[n : 2 * n], refs[2 * n :]):
        copies += fetch(src, dst, sems)
    begin(copies)
    finish(copies)


def enter_kernel(part_ref, x_ref, wg_ref, wu_ref, next_ref, g_ref, u_ref, kept_ref, sems):
    copies = fetch(next_ref, kept_ref, sems)
    begin(copies)
    k = x_ref.shape[1]
    first = pl.multiple_of(part_ref[0] * k, 128)
    for j in range(0, g_ref.shape[1], STEP):
        c = slice(j, j + STEP)
        g_ref[:, c] = dot_nn(x_ref[...], wg_ref[pl.ds(first, k), c])
        u_ref[:, c] = dot_nn(x_ref[...], wu_ref[pl.ds(first, k), c])
    finish(copies)


def hidden_kernel(part_ref, x_ref, wg_ref, wu_ref, g0_ref, u0_ref, h_ref, a_ref, b_ref):
    k = x_ref.shape[1]
    first = pl.multiple_of(part_ref[0] * k, 128)
    for j in range(0, h_ref.shape[1], STEP):
        c = slice(j, j + STEP)
        g = g0_ref[:, c] + dot_nn(x_ref[...], wg_ref[pl.ds(first, k), c])
        u = u0_ref[:, c] + dot_nn(x_ref[...], wu_ref[pl.ds(first, k), c])
        sig = jax.nn.sigmoid(g)
        gated = g * sig
        h_ref[:, c] = (gated * u).astype(BF16)
        a_ref[:, c] = (u * sig * (1.0 + g * (1.0 - sig))).astype(BF16)
        b_ref[:, c] = gated.astype(BF16)


def leave_kernel(part_ref, h_ref, w_ref, y_ref):
    n = y_ref.shape[1]
    first = part_ref[0] * n
    for j in range(0, n, STEP):
        cols = pl.ds(pl.multiple_of(first + j, 128), STEP)
        y_ref[:, j : j + STEP] = dot_nn(h_ref[...], w_ref[:, cols]).astype(y_ref.dtype)


def back_kernel(part_ref, dy_ref, w_ref, ng_ref, nu_ref, dh_ref, kg_ref, ku_ref, g_sems, u_sems):
    copies = fetch(ng_ref, kg_ref, g_sems) + fetch(nu_ref, ku_ref, u_sems)
    begin(copies)
    k = dy_ref.shape[1]
    cols = pl.ds(pl.multiple_of(part_ref[0] * k, 128), k)
    for j in range(0, dh_ref.shape[1], STEP):
        dh_ref[:, j : j + STEP] = dot_nt(dy_ref[...], w_ref[j : j + STEP, cols])
    finish(copies)


def inner_kernel(part_ref, dy_ref, w_ref, dh0_ref, a_ref, b_ref, dg_ref, du_ref):
    k = dy_ref.shape[1]
    cols = pl.ds(pl.multiple_of(part_ref[0] * k, 128), k)
    for j in range(0, dg_ref.shape[1], STEP):
        c = slice(j, j + STEP)
        dh = dh0_ref[:, c] + dot_nt(dy_ref[...], w_ref[c, cols])
        dg_ref[:, c] = (dh * a_ref[:, c].astype(F32)).astype(BF16)
        du_ref[:, c] = (dh * b_ref[:, c].astype(F32)).astype(BF16)


def input_kernel(part_ref, dg_ref, du_ref, wg_ref, wu_ref, dx_ref):
    n = dx_ref.shape[1]
    first = part_ref[0] * n
    for j in range(0, n, STEP):
        rows = pl.ds(pl.multiple_of(first + j, 128), STEP)
        dx_ref[:, j : j + STEP] = (
            dot_nt(dg_ref[...], wg_ref[rows, :]) + dot_nt(du_ref[...], wu_ref[rows, :])
        ).astype(dx_ref.dtype)


def in_hbm(x):
    return pltpu.with_memory_space_constraint(x, pltpu.HBM)


def call(kernel, outs, *args, specs=None, out_specs=None, scratch=(), flops=0, mib=6):
    kinds = {True: pltpu.VMEM, None: pltpu.HBM, False: jax.ShapeDtypeStruct}
    shapes = [kinds[kept](s, d) for s, d, kept in outs]
    moved = sum(a.size * a.dtype.itemsize for a in args) + sum(
        math.prod(s) * jnp.dtype(d).itemsize for s, d, _ in outs
    )
    result = pl.pallas_call(
        kernel,
        in_specs=specs or [SMEM] + [VMEM] * (len(args) - 1),
        out_specs=out_specs or [VMEM] * len(shapes),
        out_shape=shapes,
        scratch_shapes=list(scratch),
        compiler_params=params(mib),
        cost_estimate=cost(flops, moved),
    )(*args)
    return result if len(shapes) > 1 else result[0]


def load(*arrays):
    kept = call(
        load_kernel, [(a.shape, a.dtype, True) for a in arrays], *arrays,
        specs=[ANY] * len(arrays), scratch=[DMAS] * len(arrays),
    )
    return kept


def sems(n):
    return pltpu.SemaphoreType.DMA((n,))


def swap(x):
    return lax.ppermute(x, "dp", [(0, 1), (1, 0)])


def exchange(x, experts):
    rows, width = x.shape
    x = lax.all_to_all(
        x.reshape(experts, rows // experts, width), "expert", 0, 0, tiled=True
    )
    return x.reshape(rows, width)


def paired(tokens, expert_ids, gate_values, tiles, w_gate, w_up, w_down, grad_out):
    experts = lax.axis_size("expert")
    tok, width = tokens.shape
    top = expert_ids.shape[1]
    queue = experts * SLOTS
    half = width // 2
    wg, wu, wd = (in_hbm(w[0]) for w in (w_gate, w_up, w_down))
    hid = wg.shape[1]
    me = lax.axis_index("dp").astype(jnp.int32)
    mine = me.reshape(1)
    other = 1 - mine
    ids_t, gates_t = expert_ids.T, gate_values.T
    unit = 2 * queue * half * hid

    rows_v = pltpu.VMEM((queue, half), BF16)
    outs_v = pltpu.VMEM((tok, half), BF16)
    send, pick, weight = call(
        dispatch_kernel,
        [((queue, half), BF16, None), ((queue, tok), BF16, None), ((queue, tok), F32, None)],
        mine, tiles, in_hbm(ids_t), in_hbm(gates_t), in_hbm(tokens),
        specs=[SMEM] * 2 + [ANY] * 3, out_specs=[ANY] * 3,
        scratch=[pltpu.VMEM((top, tok), jnp.int32), pltpu.VMEM((top, tok), F32), outs_v, rows_v]
        + [pltpu.VMEM((queue, tok), BF16), pltpu.VMEM((queue, tok), F32), sems(4), sems(PIECES), sems(PIECES)],
        flops=2 * queue * tok * half,
    )
    x_own = exchange(send, experts)
    dy_send = call(
        cotangent_kernel, [((queue, half), BF16, False)], pick, weight, grad_out,
        specs=[VMEM] * 3, flops=2 * queue * tok * half,
    )
    dy_send, x_own = lax.optimization_barrier((dy_send, x_own))
    dy_own = exchange(dy_send, experts)

    inner = ((queue, hid), F32, True)
    x_oth = swap(x_own)
    wg0, wu0 = load(wg, wu)
    g0, u0, wd0 = call(
        enter_kernel, [inner, inner, (wd.shape, BF16, True)], mine, x_own, wg0, wu0, wd,
        specs=[SMEM] + [VMEM] * 3 + [ANY], scratch=[DMAS], flops=2 * unit,
    )
    h, a, b = call(
        hidden_kernel, [((queue, hid), BF16, False)] * 3, other, x_oth, wg0, wu0, g0, u0,
        flops=2 * unit,
    )
    y_far = call(leave_kernel, [((queue, half), BF16, False)], other, h, wd0, flops=unit)
    y_far = swap(y_far)
    y_near = call(leave_kernel, [((queue, half), F32, False)], mine, h, wd0, flops=unit)
    y_sum = call(sum_kernel, [((queue, half), BF16, None)], y_near, y_far, specs=[VMEM] * 2)
    y_back = exchange(y_sum, experts)

    dy_oth = swap(dy_own)
    wd1 = load(wd)
    dh0, wg1, wu1 = call(
        back_kernel, [inner, (wg.shape, BF16, True), (wu.shape, BF16, True)], mine, dy_own, wd1, wg, wu,
        specs=[SMEM] + [VMEM] * 2 + [ANY] * 2, scratch=[DMAS] * 2, flops=unit,
    )
    dg, du = call(
        inner_kernel, [((queue, hid), BF16, False)] * 2, other, dy_oth, wd1, dh0, a, b,
        flops=unit,
    )
    dx_far = call(input_kernel, [((queue, half), BF16, False)], other, dg, du, wg1, wu1, flops=2 * unit)
    dx_far = swap(dx_far)
    dx_near = call(input_kernel, [((queue, half), F32, False)], mine, dg, du, wg1, wu1, flops=2 * unit)
    dx_sum = call(sum_kernel, [((queue, half), BF16, None)], dx_near, dx_far, specs=[VMEM] * 2)
    dx_back = exchange(dx_sum, experts)

    blocks = 2
    wide = half // blocks
    keep = lambda i, s: (0, 0)
    own = lambda i, s: (0, jnp.minimum(i, blocks - 1))
    oth = lambda i, s: (0, jnp.maximum(i - blocks, 0))
    place = lambda i, s: jnp.where(i < blocks, s[0] * blocks + i, (1 - s[0]) * blocks + i - blocks)

    def gradients(kernel, ins, halves, whole, out_spec, shapes):
        return pl.pallas_call(
            kernel,
            grid_spec=pltpu.PrefetchScalarGridSpec(
                num_scalar_prefetch=1,
                grid=(2 * blocks,),
                in_specs=[pl.BlockSpec((queue, wide), own), pl.BlockSpec((queue, wide), oth)]
                + [pl.BlockSpec((queue, hid), keep)] * len(whole),
                out_specs=[out_spec] * len(shapes),
            ),
            out_shape=shapes,
            compiler_params=params(40),
            cost_estimate=cost(2 * unit * len(shapes), 2 * width * hid * len(shapes)),
        )(ins, *(in_hbm(v) for v in (*halves, *whole)))

    grad_gate, grad_up = gradients(
        columns_kernel, mine, (x_own, x_oth), (dg, du),
        pl.BlockSpec((wide, hid), lambda i, s: (place(i, s), 0)),
        [jax.ShapeDtypeStruct((width, hid), BF16)] * 2,
    )

    (grad_down,) = gradients(
        rows_kernel, mine, (dy_own, dy_oth), (h,),
        pl.BlockSpec((hid, wide), lambda i, s: (0, place(i, s))),
        [jax.ShapeDtypeStruct((hid, width), BF16)],
    )

    mixed, score = call(
        combine_kernel, [((tok, half), BF16, None), ((top, tok), F32, False)],
        pick, weight, ids_t, in_hbm(y_back), grad_out,
        specs=[VMEM] * 3 + [ANY, VMEM], out_specs=[ANY, VMEM],
        scratch=[rows_v, outs_v, sems(PIECES), sems(PIECES)],
        mib=8, flops=6 * queue * tok * half,
    )
    grad_gates = (score + swap(score)).T
    grad_tokens = call(
        spread_kernel, [((tok, half), BF16, False)], pick, dx_back,
        specs=[VMEM] * 2, flops=2 * queue * tok * half,
    )
    return mixed, grad_tokens, grad_gates, grad_gate[None], grad_up[None], grad_down[None]


def route_tables(ids, gates, count, experts, slots, tile):
    tok, top = ids.shape
    queue = experts * slots
    live = jnp.arange(tok, dtype=jnp.int32) < count * tile
    valid = (ids < experts) & live[:, None]
    flat_ids = ids.reshape(-1)
    flat_valid = valid.reshape(-1)
    onehot = (
        (flat_ids[:, None] == jnp.arange(experts, dtype=jnp.int32)[None, :]) & flat_valid[:, None]
    ).astype(jnp.int32)
    ranks = jnp.sum((jnp.cumsum(onehot, axis=0) - 1) * onehot, axis=1)
    target = jnp.where(flat_valid, flat_ids * slots + ranks, -1)
    match = (target[None, :] == jnp.arange(queue, dtype=jnp.int32)[:, None]).astype(F32)
    picker = jnp.sum(match.reshape(queue, tok, top), axis=2)
    slot_gate = jnp.dot(match, gates.reshape(-1), precision=lax.Precision.HIGHEST)
    return match, picker, slot_gate


def spread_rows(picker_tb, values):
    upper = values.astype(BF16)
    lower = (values - upper.astype(F32)).astype(BF16)
    return dot_nn(picker_tb, upper) + dot_nn(picker_tb, lower)


def shared(tokens, expert_ids, gate_values, tiles, w_gate, w_up, w_down, grad_out):
    experts = lax.axis_size("expert")
    groups = lax.axis_size("dp")
    tok, width = tokens.shape
    top = expert_ids.shape[1]
    columns = width // groups
    match, picker, slot_gate = route_tables(expert_ids, gate_values, tiles[0], experts, SLOTS, TILE)
    pick_b = picker.astype(BF16)
    picker_tb = picker.T.astype(BF16)
    mine = lax.dynamic_slice_in_dim(tokens, lax.axis_index("dp") * columns, columns, 1)
    rows = exchange(dot_nn(pick_b, mine).astype(BF16), experts)
    rows = lax.all_gather(rows, "dp", axis=1, tiled=True)
    w_g, w_u, w_d = w_gate[0], w_up[0], w_down[0]
    gate_pre = dot_nn(rows, w_g)
    up_pre = dot_nn(rows, w_u)
    sig = jax.nn.sigmoid(gate_pre)
    hidden = (gate_pre * sig * up_pre).astype(BF16)
    summed = lax.psum_scatter(
        dot_nn(hidden, w_d).astype(BF16), "dp", scatter_dimension=1, tiled=True
    )
    returned = exchange(summed, experts).astype(F32)
    mixed = spread_rows(picker_tb, returned * slot_gate[:, None]).astype(BF16)
    dy_rows = dot_nn(pick_b, grad_out)
    score = lax.psum(jnp.sum(dy_rows * returned, axis=1), "dp")
    dy_own = exchange((dy_rows * slot_gate[:, None]).astype(BF16), experts)
    dy_slots = lax.all_gather(dy_own, "dp", axis=1, tiled=True)
    d_hidden = dot_nt(dy_slots, w_d)
    d_gate = (d_hidden * up_pre * sig * (1.0 + gate_pre * (1.0 - sig))).astype(BF16)
    d_up = (d_hidden * gate_pre * sig).astype(BF16)
    grad_down = dot_tn(hidden, dy_slots).astype(BF16)
    grad_gate = dot_tn(rows, d_gate).astype(BF16)
    grad_up = dot_tn(rows, d_up).astype(BF16)
    input_rows = dot_nt(d_gate, w_g) + dot_nt(d_up, w_u)
    input_summed = lax.psum_scatter(
        input_rows.astype(BF16), "dp", scatter_dimension=1, tiled=True
    )
    grad_tokens = dot_nn(picker_tb, exchange(input_summed, experts)).astype(BF16)
    grad_gates = jnp.dot(score, match, precision=lax.Precision.HIGHEST).reshape(tok, top)
    return mixed, grad_tokens, grad_gates, grad_gate[None], grad_up[None], grad_down[None]


def in_pairs(mesh, width, hid):
    return mesh.shape["dp"] == 2 and width % (2 * STEP) == 0 and hid % (2 * STEP) == 0


def solution(mesh):
    placed = (
        P("expert", None),
        P("expert", None),
        P("expert", None),
        P("expert"),
        P("expert", None, "dp"),
        P("expert", None, "dp"),
        P("expert", "dp", None),
        P("expert", "dp"),
    )
    over = functools.partial(
        jax.shard_map,
        mesh=mesh,
        in_specs=placed,
        out_specs=(
            P("expert", "dp"),
            P("expert", "dp"),
            P("expert", None),
            P("expert", None, "dp"),
            P("expert", None, "dp"),
            P("expert", "dp", None),
        ),
        check_vma=False,
    )

    def layer(*args):
        if not in_pairs(mesh, *args[4].shape[1:]):
            return over(shared)(*args)
        return over(paired)(*args)

    return layer
```

```python
import functools
import math

import jax
import jax.numpy as jnp
from jax import lax
from jax.experimental import pallas as pl
from jax.experimental.pallas import tpu as pltpu
from jax.sharding import PartitionSpec as P


TILE = 128
SLOTS = 16
F32 = jnp.float32
BF16 = jnp.bfloat16
VMEM = pl.BlockSpec(memory_space=pltpu.VMEM)
ANY = pl.BlockSpec(memory_space=pl.ANY)
SMEM = pl.BlockSpec(memory_space=pltpu.SMEM)
STEP = 256
PARTS = 4
PIECES = 2
DMAS = pltpu.SemaphoreType.DMA((PARTS,))


def params(mib):
    return pltpu.CompilerParams(vmem_limit_bytes=mib << 20)


def cost(flops, moved):
    return pl.CostEstimate(flops=flops, bytes_accessed=moved, transcendentals=0)


def dot_nn(a, b):
    return jnp.dot(a, b, preferred_element_type=F32)


def dot_nt(a, b):
    return lax.dot_general(a, b, (((1,), (1,)), ((), ())), preferred_element_type=F32)


def dot_tn(a, b):
    return lax.dot_general(a, b, (((0,), (0,)), ((), ())), preferred_element_type=F32)


def pieces(src, dst, sems, src_first=0, dst_first=0):
    wide = min(src.shape[1], dst.shape[1]) // PIECES
    return [
        pltpu.make_async_copy(
            src.at[:, pl.ds(pl.multiple_of(src_first + i * wide, 128), wide)],
            dst.at[:, pl.ds(pl.multiple_of(dst_first + i * wide, 128), wide)],
            sems.at[i],
        )
        for i in range(PIECES)
    ]


def dispatch_kernel(
    part_ref, tiles_ref, ids_ref, gates_ref, tok_ref, send_ref, pick_ref, weight_ref,
    ids_v, gates_v, tok_v, send_v, pick_v, weight_v, near_s, in_s, out_s,
):
    top, tok = ids_v.shape
    queue, half = send_v.shape
    named_in = [
        pltpu.make_async_copy(ids_ref, ids_v, near_s.at[0]),
        pltpu.make_async_copy(gates_ref, gates_v, near_s.at[1]),
    ]
    tables = [
        pltpu.make_async_copy(pick_v, pick_ref, near_s.at[2]),
        pltpu.make_async_copy(weight_v, weight_ref, near_s.at[3]),
    ]
    ins = pieces(tok_ref, tok_v, in_s, part_ref[0] * half)
    outs = pieces(send_v, send_ref, out_s)
    begin(named_in + ins)
    owner = lax.broadcasted_iota(jnp.int32, (queue, tok), 0)
    expert, slot = owner // SLOTS, owner % SLOTS
    before = lax.broadcasted_iota(jnp.int32, (tok, tok), 0) < lax.broadcasted_iota(
        jnp.int32, (tok, tok), 1
    )
    earlier = jnp.where(before, 1.0, 0.0).astype(BF16)
    live = lax.broadcasted_iota(jnp.int32, (1, tok), 1) < tiles_ref[0] * TILE
    finish(named_in)
    ids = jnp.where(live, ids_v[...], -1)
    gates = gates_v[...]
    named = jnp.zeros((queue, tok), F32)
    weight = jnp.zeros((queue, tok), F32)
    for k in range(top):
        hit = jnp.broadcast_to(ids[k : k + 1, :], (queue, tok)) == expert
        named = jnp.where(hit, 1.0, named)
        weight = jnp.where(hit, jnp.broadcast_to(gates[k : k + 1, :], (queue, tok)), weight)
    rank = dot_nn(named.astype(BF16), earlier)
    chosen = (named > 0.5) & (rank == slot.astype(F32))
    pick = jnp.where(chosen, 1.0, 0.0).astype(BF16)
    pick_v[...] = pick
    weight_v[...] = jnp.where(chosen, weight, 0.0)
    begin(tables)
    wide = half // PIECES
    for i in range(PIECES):
        c = slice(i * wide, (i + 1) * wide)
        ins[i].wait()
        send_v[:, c] = dot_nn(pick, tok_v[:, c]).astype(BF16)
        outs[i].start()
    finish(outs + tables)


def cotangent_kernel(pick_ref, weight_ref, out_ref, send_ref):
    gate = jnp.sum(weight_ref[...], axis=1, keepdims=True)
    send_ref[...] = (dot_nn(pick_ref[...], out_ref[...]) * gate).astype(BF16)


def combine_kernel(
    pick_ref, weight_ref, ids_ref, back_ref, out_ref, mixed_ref, score_ref, turned_ref,
    back_v, mixed_v, in_s, out_s,
):
    ins, outs = pieces(back_ref, back_v, in_s), pieces(mixed_v, mixed_ref, out_s)
    begin(ins)
    weight = weight_ref[...].T
    upper = weight.astype(BF16)
    lower = (weight - upper.astype(F32)).astype(BF16)
    wide = back_v.shape[1] // PIECES
    pairs = 0.0
    for i in range(PIECES):
        c = slice(i * wide, (i + 1) * wide)
        ins[i].wait()
        back = back_v[:, c]
        mixed_v[:, c] = (dot_nn(upper, back) + dot_nn(lower, back)).astype(BF16)
        outs[i].start()
        pairs += dot_nt(back, out_ref[:, c])
    pick = pick_ref[...].astype(F32)
    turned_ref[...] = pick.T.astype(BF16)
    pairs = jnp.where(pick > 0.5, pairs, 0.0)
    queue, tok = pairs.shape
    expert = lax.broadcasted_iota(jnp.int32, (queue, tok), 0) // SLOTS
    ids = ids_ref[...]
    for k in range(ids.shape[0]):
        hit = jnp.broadcast_to(ids[k : k + 1, :], (queue, tok)) == expert
        score_ref[k : k + 1, :] = jnp.sum(jnp.where(hit, pairs, 0.0), axis=0, keepdims=True)
    finish(outs)


def spread_kernel(turned_ref, back_ref, out_ref, out_v, out_s):
    outs = pieces(out_v, out_ref, out_s)
    wide = out_v.shape[1] // PIECES
    for i in range(PIECES):
        c = slice(i * wide, (i + 1) * wide)
        out_v[:, c] = dot_nn(turned_ref[...], back_ref[:, c]).astype(BF16)
        outs[i].start()
    finish(outs)


def sum_kernel(near_ref, far_ref, out_ref):
    out_ref[...] = (near_ref[...] + far_ref[...].astype(F32)).astype(BF16)


def columns_kernel(part_ref, own_ref, oth_ref, dg_ref, du_ref, gate_ref, up_ref):
    def write(x):
        turned = x.T
        gate_ref[...] = dot_nn(turned, dg_ref[...]).astype(BF16)
        up_ref[...] = dot_nn(turned, du_ref[...]).astype(BF16)

    near = pl.program_id(0) < pl.num_programs(0) // 2

    @pl.when(near)
    def _():
        write(own_ref[...])

    @pl.when(jnp.logical_not(near))
    def _():
        write(oth_ref[...])


def rows_kernel(part_ref, own_ref, oth_ref, h_ref, down_ref):
    turned = h_ref[...].T
    near = pl.program_id(0) < pl.num_programs(0) // 2

    @pl.when(near)
    def _():
        down_ref[...] = dot_nn(turned, own_ref[...]).astype(BF16)

    @pl.when(jnp.logical_not(near))
    def _():
        down_ref[...] = dot_nn(turned, oth_ref[...]).astype(BF16)


def fetch(src, dst, sems):
    rows = src.shape[0] // PARTS
    return [
        pltpu.make_async_copy(src.at[pl.ds(i * rows, rows)], dst.at[pl.ds(i * rows, rows)], sems.at[i])
        for i in range(PARTS)
    ]


def begin(copies):
    for copy in copies:
        copy.start()


def finish(copies):
    for copy in copies:
        copy.wait()


def load_kernel(*refs):
    n = len(refs) // 3
    copies = []
    for src, dst, sems in zip(refs[:n], refs[n : 2 * n], refs[2 * n :]):
        copies += fetch(src, dst, sems)
    begin(copies)
    finish(copies)


def enter_kernel(part_ref, x_ref, wg_ref, wu_ref, next_ref, g_ref, u_ref, kept_ref, sems):
    copies = fetch(next_ref, kept_ref, sems)
    begin(copies)
    k = x_ref.shape[1]
    first = pl.multiple_of(part_ref[0] * k, 128)
    for j in range(0, g_ref.shape[1], STEP):
        c = slice(j, j + STEP)
        g_ref[:, c] = dot_nn(x_ref[...], wg_ref[pl.ds(first, k), c])
        u_ref[:, c] = dot_nn(x_ref[...], wu_ref[pl.ds(first, k), c])
    finish(copies)


def hidden_kernel(part_ref, x_ref, wg_ref, wu_ref, g0_ref, u0_ref, h_ref, a_ref, b_ref):
    k = x_ref.shape[1]
    first = pl.multiple_of(part_ref[0] * k, 128)
    for j in range(0, h_ref.shape[1], STEP):
        c = slice(j, j + STEP)
        g = g0_ref[:, c] + dot_nn(x_ref[...], wg_ref[pl.ds(first, k), c])
        u = u0_ref[:, c] + dot_nn(x_ref[...], wu_ref[pl.ds(first, k), c])
        sig = jax.nn.sigmoid(g)
        gated = g * sig
        h_ref[:, c] = (gated * u).astype(BF16)
        a_ref[:, c] = (u * sig * (1.0 + g * (1.0 - sig))).astype(BF16)
        b_ref[:, c] = gated.astype(BF16)


def leave_kernel(part_ref, h_ref, w_ref, y_ref):
    n = y_ref.shape[1]
    first = part_ref[0] * n
    for j in range(0, n, STEP):
        cols = pl.ds(pl.multiple_of(first + j, 128), STEP)
        y_ref[:, j : j + STEP] = dot_nn(h_ref[...], w_ref[:, cols]).astype(y_ref.dtype)


def back_kernel(part_ref, dy_ref, w_ref, ng_ref, nu_ref, dh_ref, kg_ref, ku_ref, g_sems, u_sems):
    copies = fetch(ng_ref, kg_ref, g_sems) + fetch(nu_ref, ku_ref, u_sems)
    begin(copies)
    k = dy_ref.shape[1]
    cols = pl.ds(pl.multiple_of(part_ref[0] * k, 128), k)
    for j in range(0, dh_ref.shape[1], STEP):
        dh_ref[:, j : j + STEP] = dot_nt(dy_ref[...], w_ref[j : j + STEP, cols])
    finish(copies)


def inner_kernel(part_ref, dy_ref, w_ref, dh0_ref, a_ref, b_ref, dg_ref, du_ref):
    k = dy_ref.shape[1]
    cols = pl.ds(pl.multiple_of(part_ref[0] * k, 128), k)
    for j in range(0, dg_ref.shape[1], STEP):
        c = slice(j, j + STEP)
        dh = dh0_ref[:, c] + dot_nt(dy_ref[...], w_ref[c, cols])
        dg_ref[:, c] = (dh * a_ref[:, c].astype(F32)).astype(BF16)
        du_ref[:, c] = (dh * b_ref[:, c].astype(F32)).astype(BF16)


def input_kernel(part_ref, dg_ref, du_ref, wg_ref, wu_ref, dx_ref):
    n = dx_ref.shape[1]
    first = part_ref[0] * n
    for j in range(0, n, STEP):
        rows = pl.ds(pl.multiple_of(first + j, 128), STEP)
        dx_ref[:, j : j + STEP] = (
            dot_nt(dg_ref[...], wg_ref[rows, :]) + dot_nt(du_ref[...], wu_ref[rows, :])
        ).astype(dx_ref.dtype)


def in_hbm(x):
    return pltpu.with_memory_space_constraint(x, pltpu.HBM)


def call(kernel, outs, *args, specs=None, out_specs=None, scratch=(), flops=0, mib=6):
    kinds = {True: pltpu.VMEM, None: pltpu.HBM, False: jax.ShapeDtypeStruct}
    shapes = [kinds[kept](s, d) for s, d, kept in outs]
    moved = sum(a.size * a.dtype.itemsize for a in args) + sum(
        math.prod(s) * jnp.dtype(d).itemsize for s, d, _ in outs
    )
    result = pl.pallas_call(
        kernel,
        in_specs=specs or [SMEM] + [VMEM] * (len(args) - 1),
        out_specs=out_specs or [VMEM] * len(shapes),
        out_shape=shapes,
        scratch_shapes=list(scratch),
        compiler_params=params(mib),
        cost_estimate=cost(flops, moved),
    )(*args)
    return result if len(shapes) > 1 else result[0]


def load(*arrays):
    kept = call(
        load_kernel, [(a.shape, a.dtype, True) for a in arrays], *arrays,
        specs=[ANY] * len(arrays), scratch=[DMAS] * len(arrays),
    )
    return kept


def sems(n):
    return pltpu.SemaphoreType.DMA((n,))


def swap(x):
    return lax.ppermute(x, "dp", [(0, 1), (1, 0)])


def exchange(x, experts):
    rows, width = x.shape
    x = lax.all_to_all(
        x.reshape(experts, rows // experts, width), "expert", 0, 0, tiled=True
    )
    return x.reshape(rows, width)


def paired(tokens, expert_ids, gate_values, tiles, w_gate, w_up, w_down, grad_out):
    experts = lax.axis_size("expert")
    tok, width = tokens.shape
    top = expert_ids.shape[1]
    queue = experts * SLOTS
    half = width // 2
    wg, wu, wd = (in_hbm(w[0]) for w in (w_gate, w_up, w_down))
    hid = wg.shape[1]
    me = lax.axis_index("dp").astype(jnp.int32)
    mine = me.reshape(1)
    other = 1 - mine
    ids_t, gates_t = expert_ids.T, gate_values.T
    unit = 2 * queue * half * hid

    rows_v = pltpu.VMEM((queue, half), BF16)
    outs_v = pltpu.VMEM((tok, half), BF16)
    send, pick, weight = call(
        dispatch_kernel,
        [((queue, half), BF16, None), ((queue, tok), BF16, None), ((queue, tok), F32, None)],
        mine, tiles, in_hbm(ids_t), in_hbm(gates_t), in_hbm(tokens),
        specs=[SMEM] * 2 + [ANY] * 3, out_specs=[ANY] * 3,
        scratch=[pltpu.VMEM((top, tok), jnp.int32), pltpu.VMEM((top, tok), F32), outs_v, rows_v]
        + [pltpu.VMEM((queue, tok), BF16), pltpu.VMEM((queue, tok), F32), sems(4), sems(PIECES), sems(PIECES)],
        flops=2 * queue * tok * half,
    )
    x_own = exchange(send, experts)
    dy_send = call(
        cotangent_kernel, [((queue, half), BF16, False)], pick, weight, grad_out,
        specs=[VMEM] * 3, flops=2 * queue * tok * half,
    )
    dy_send, x_own = lax.optimization_barrier((dy_send, x_own))
    dy_own = exchange(dy_send, experts)

    inner = ((queue, hid), F32, True)
    x_oth = swap(x_own)
    wg0, wu0 = load(wg, wu)
    g0, u0, wd0 = call(
        enter_kernel, [inner, inner, (wd.shape, BF16, True)], mine, x_own, wg0, wu0, wd,
        specs=[SMEM] + [VMEM] * 3 + [ANY], scratch=[DMAS], flops=2 * unit,
    )
    h, a, b = call(
        hidden_kernel, [((queue, hid), BF16, False)] * 3, other, x_oth, wg0, wu0, g0, u0,
        flops=2 * unit,
    )
    y_far = call(leave_kernel, [((queue, half), BF16, False)], other, h, wd0, flops=unit)
    y_far = swap(y_far)
    y_near = call(leave_kernel, [((queue, half), F32, False)], mine, h, wd0, flops=unit)
    y_sum = call(sum_kernel, [((queue, half), BF16, None)], y_near, y_far, specs=[VMEM] * 2)
    y_back = exchange(y_sum, experts)

    dy_oth = swap(dy_own)
    wd1 = load(wd)
    dh0, wg1, wu1 = call(
        back_kernel, [inner, (wg.shape, BF16, True), (wu.shape, BF16, True)], mine, dy_own, wd1, wg, wu,
        specs=[SMEM] + [VMEM] * 2 + [ANY] * 2, scratch=[DMAS] * 2, flops=unit,
    )
    dg, du = call(
        inner_kernel, [((queue, hid), BF16, False)] * 2, other, dy_oth, wd1, dh0, a, b,
        flops=unit,
    )
    dx_far = call(input_kernel, [((queue, half), BF16, False)], other, dg, du, wg1, wu1, flops=2 * unit)
    dx_far = swap(dx_far)
    dx_near = call(input_kernel, [((queue, half), F32, False)], mine, dg, du, wg1, wu1, flops=2 * unit)
    dx_sum = call(sum_kernel, [((queue, half), BF16, None)], dx_near, dx_far, specs=[VMEM] * 2)
    dx_back = exchange(dx_sum, experts)

    blocks = 2
    wide = half // blocks
    keep = lambda i, s: (0, 0)
    own = lambda i, s: (0, jnp.minimum(i, blocks - 1))
    oth = lambda i, s: (0, jnp.maximum(i - blocks, 0))
    place = lambda i, s: jnp.where(i < blocks, s[0] * blocks + i, (1 - s[0]) * blocks + i - blocks)

    def gradients(kernel, ins, halves, whole, out_spec, shapes):
        return pl.pallas_call(
            kernel,
            grid_spec=pltpu.PrefetchScalarGridSpec(
                num_scalar_prefetch=1,
                grid=(2 * blocks,),
                in_specs=[pl.BlockSpec((queue, wide), own), pl.BlockSpec((queue, wide), oth)]
                + [pl.BlockSpec((queue, hid), keep)] * len(whole),
                out_specs=[out_spec] * len(shapes),
            ),
            out_shape=shapes,
            compiler_params=params(40),
            cost_estimate=cost(2 * unit * len(shapes), 2 * width * hid * len(shapes)),
        )(ins, *(in_hbm(v) for v in (*halves, *whole)))

    grad_gate, grad_up = gradients(
        columns_kernel, mine, (x_own, x_oth), (dg, du),
        pl.BlockSpec((wide, hid), lambda i, s: (place(i, s), 0)),
        [jax.ShapeDtypeStruct((width, hid), BF16)] * 2,
    )

    (grad_down,) = gradients(
        rows_kernel, mine, (dy_own, dy_oth), (h,),
        pl.BlockSpec((hid, wide), lambda i, s: (0, place(i, s))),
        [jax.ShapeDtypeStruct((hid, width), BF16)],
    )

    mixed, score, turned = call(
        combine_kernel,
        [((tok, half), BF16, None), ((top, tok), F32, False), ((tok, queue), BF16, False)],
        pick, weight, ids_t, in_hbm(y_back), grad_out,
        specs=[VMEM] * 3 + [ANY, VMEM], out_specs=[ANY, VMEM, VMEM],
        scratch=[rows_v, outs_v, sems(PIECES), sems(PIECES)],
        mib=8, flops=6 * queue * tok * half,
    )
    grad_gates = (score + swap(score)).T
    grad_tokens = call(
        spread_kernel, [((tok, half), BF16, None)], turned, dx_back,
        specs=[VMEM] * 2, out_specs=[ANY], scratch=[outs_v, sems(PIECES)],
        flops=2 * queue * tok * half,
    )
    return mixed, grad_tokens, grad_gates, grad_gate[None], grad_up[None], grad_down[None]


def route_tables(ids, gates, count, experts, slots, tile):
    tok, top = ids.shape
    queue = experts * slots
    live = jnp.arange(tok, dtype=jnp.int32) < count * tile
    valid = (ids < experts) & live[:, None]
    flat_ids = ids.reshape(-1)
    flat_valid = valid.reshape(-1)
    onehot = (
        (flat_ids[:, None] == jnp.arange(experts, dtype=jnp.int32)[None, :]) & flat_valid[:, None]
    ).astype(jnp.int32)
    ranks = jnp.sum((jnp.cumsum(onehot, axis=0) - 1) * onehot, axis=1)
    target = jnp.where(flat_valid, flat_ids * slots + ranks, -1)
    match = (target[None, :] == jnp.arange(queue, dtype=jnp.int32)[:, None]).astype(F32)
    picker = jnp.sum(match.reshape(queue, tok, top), axis=2)
    slot_gate = jnp.dot(match, gates.reshape(-1), precision=lax.Precision.HIGHEST)
    return match, picker, slot_gate


def spread_rows(picker_tb, values):
    upper = values.astype(BF16)
    lower = (values - upper.astype(F32)).astype(BF16)
    return dot_nn(picker_tb, upper) + dot_nn(picker_tb, lower)


def shared(tokens, expert_ids, gate_values, tiles, w_gate, w_up, w_down, grad_out):
    experts = lax.axis_size("expert")
    groups = lax.axis_size("dp")
    tok, width = tokens.shape
    top = expert_ids.shape[1]
    columns = width // groups
    match, picker, slot_gate = route_tables(expert_ids, gate_values, tiles[0], experts, SLOTS, TILE)
    pick_b = picker.astype(BF16)
    picker_tb = picker.T.astype(BF16)
    mine = lax.dynamic_slice_in_dim(tokens, lax.axis_index("dp") * columns, columns, 1)
    rows = exchange(dot_nn(pick_b, mine).astype(BF16), experts)
    rows = lax.all_gather(rows, "dp", axis=1, tiled=True)
    w_g, w_u, w_d = w_gate[0], w_up[0], w_down[0]
    gate_pre = dot_nn(rows, w_g)
    up_pre = dot_nn(rows, w_u)
    sig = jax.nn.sigmoid(gate_pre)
    hidden = (gate_pre * sig * up_pre).astype(BF16)
    summed = lax.psum_scatter(
        dot_nn(hidden, w_d).astype(BF16), "dp", scatter_dimension=1, tiled=True
    )
    returned = exchange(summed, experts).astype(F32)
    mixed = spread_rows(picker_tb, returned * slot_gate[:, None]).astype(BF16)
    dy_rows = dot_nn(pick_b, grad_out)
    score = lax.psum(jnp.sum(dy_rows * returned, axis=1), "dp")
    dy_own = exchange((dy_rows * slot_gate[:, None]).astype(BF16), experts)
    dy_slots = lax.all_gather(dy_own, "dp", axis=1, tiled=True)
    d_hidden = dot_nt(dy_slots, w_d)
    d_gate = (d_hidden * up_pre * sig * (1.0 + gate_pre * (1.0 - sig))).astype(BF16)
    d_up = (d_hidden * gate_pre * sig).astype(BF16)
    grad_down = dot_tn(hidden, dy_slots).astype(BF16)
    grad_gate = dot_tn(rows, d_gate).astype(BF16)
    grad_up = dot_tn(rows, d_up).astype(BF16)
    input_rows = dot_nt(d_gate, w_g) + dot_nt(d_up, w_u)
    input_summed = lax.psum_scatter(
        input_rows.astype(BF16), "dp", scatter_dimension=1, tiled=True
    )
    grad_tokens = dot_nn(picker_tb, exchange(input_summed, experts)).astype(BF16)
    grad_gates = jnp.dot(score, match, precision=lax.Precision.HIGHEST).reshape(tok, top)
    return mixed, grad_tokens, grad_gates, grad_gate[None], grad_up[None], grad_down[None]


def in_pairs(mesh, width, hid):
    return mesh.shape["dp"] == 2 and width % (2 * STEP) == 0 and hid % (2 * STEP) == 0


def solution(mesh):
    placed = (
        P("expert", None),
        P("expert", None),
        P("expert", None),
        P("expert"),
        P("expert", None, "dp"),
        P("expert", None, "dp"),
        P("expert", "dp", None),
        P("expert", "dp"),
    )
    over = functools.partial(
        jax.shard_map,
        mesh=mesh,
        in_specs=placed,
        out_specs=(
            P("expert", "dp"),
            P("expert", "dp"),
            P("expert", None),
            P("expert", None, "dp"),
            P("expert", None, "dp"),
            P("expert", "dp", None),
        ),
        check_vma=False,
    )

    def layer(*args):
        if not in_pairs(mesh, *args[4].shape[1:]):
            return over(shared)(*args)
        return over(paired)(*args)

    return layer
```
